32 devices in a mesh: row: 16 (over z, x, core), col: 2 (over y).
Axes of the slice: x: 2, y: 2, z: 4, core: 2. Of those that a mesh axis runs over, the one named last changes fastest.
Arguments:
- dosage: bfloat16 [128, 24576], P(('row', 'col')), may hold values from 0 to 2
- phenos: bfloat16 [16, 24576], P(None, 'col'), may hold values from -6 to 6
Outputs:
- grm: float32 [24576, 24576], P('row', 'col')
- projected: float32 [16, 24576], P(None, ('row', 'col'))
The draws below stay inside these ranges and needn't reach their ends.
All inputs are finite; a program needn't handle non-finite values.
Results may differ from the reference program's by a relative error of at most 0.0049.
Values may be sent and summed in bfloat16 or wider, within the bound.
A program may use at most 192 MiB of HBM per device.

```python
import math
import jax
import jax.numpy as jnp
from jax import lax

SAMPLES = 24576
PHENOS = 16
SNPS = 128


def draw_dosage(key, part):
    key_freq, key_unif = jax.random.split(key, 2)
    freq = jnp.exp(jax.random.uniform(key_freq, (SNPS, 1), jnp.float32, math.log(0.05), math.log(0.5)))
    unif = jax.random.uniform(key_unif, (SNPS, SAMPLES), jnp.float32)
    return (4.0 * freq * unif).astype(jnp.bfloat16)


def block_scale(own_key, dims, cuts, smallest, largest):
    loudness, own = 1.0, jax.random.fold_in(own_key, 6)
    for position, parts in cuts:
        heights = jnp.exp(jax.random.uniform(jax.random.fold_in(own, position), (parts,), jnp.float32, smallest / len(cuts), largest / len(cuts)))
        loudness = loudness * jnp.repeat(heights, dims[position] // parts).reshape([-1 if axis == position else 1 for axis in range(len(dims))])
    return loudness


def gaussian(key, shape, scale, bound, cuts=(), kind=jnp.bfloat16):
    level = block_scale(key, shape, cuts, -0.22, 0.18) if cuts else 1.0
    values = jax.random.normal(key, shape, jnp.float32) * scale * level
    return jnp.minimum(jnp.maximum(values, -bound), bound).astype(kind)


def setup_inputs(seed: int = 0) -> dict:
    arg_keys = jax.random.split(jax.random.key(seed), 3)
    return {
        "dosage": draw_dosage(jax.random.fold_in(arg_keys[2], 71), 0),
        "phenos": gaussian(arg_keys[1], (PHENOS, SAMPLES), 1.0, 6.0, ((1, 2),)),
    }


eps = 1e-05

def standardize(dosage):
    values = dosage.astype(jnp.float32)
    site_mean = lax.optimization_barrier(jnp.mean(values, axis=1, keepdims=True))
    centred = values - site_mean
    site_var = lax.optimization_barrier(jnp.mean(centred * centred, axis=1, keepdims=True))
    return (centred * lax.rsqrt(site_var + eps)).astype(jnp.bfloat16)

def reference(dosage, phenos):
    standard = standardize(dosage)
    grm = jnp.dot(standard.T, standard, preferred_element_type=jnp.float32) * (1.0 / SNPS)
    grm_half = grm.astype(jnp.bfloat16)
    projected = lax.dot_general(phenos, grm_half, (((1,), (1,)), ((), ())), preferred_element_type=jnp.float32)
    return (grm, projected)
```

```python
import functools

import jax
import jax.numpy as jnp
from jax import lax
from jax.experimental import pallas as pl
from jax.experimental.pallas import tpu as pltpu
from jax.sharding import PartitionSpec as P

eps = 1e-05
MESH = pl.DeviceIdType.MESH


def place_of(row, depth, width):
    chip, core = row // 2, row % 2
    a, b = chip // width, chip % width
    turn = depth - 1 - a
    odd = turn % 2
    first = (width - 1 - b) // (width - 1)
    later = depth + turn * (width - 1) + (1 - odd) * (b - 1) + odd * (width - 1 - b)
    return first * a + (1 - first) * later, core


def chip_at(place, depth, width):
    first = 1 - jnp.minimum(place // depth, 1)
    rest = jnp.maximum(place - depth, 0)
    turn, step = rest // (width - 1), rest % (width - 1)
    odd = turn % 2
    later = (depth - 1 - turn) * width + (1 - odd) * (1 + step) + odd * (width - 1 - step)
    return first * place * width + (1 - first) * later


def gather_kernel(
    rows, cols, halves, dosage_ref, phenos_ref, col_ref, row_ref, share_ref,
    raw, traits, mine, pieces,
    load, swap_send, swap_recv, first_send, first_recv, ring_send, ring_recv, sib_send, sib_recv,
    line_send, line_recv, share_send, share_recv,
):
    row, col = lax.axis_index("row"), lax.axis_index("col")
    chips = rows // 2
    depth = min(4, chips)
    width = chips // depth
    place, core = place_of(row, depth, width)
    sibling = row + 1 - 2 * core
    def row_away(shift, which):
        there = (place + (chips - shift) * (1 - core) + shift * core) % chips
        return chip_at(there, depth, width) * 2 + which

    upstream = row_away(1, core)
    downstream = row_away(chips - 1, core)
    sites, samples = dosage_ref.shape
    wide, tall = col_ref.shape[2], row_ref.shape[2]
    part = wide // halves
    per_col = rows // cols
    home = row // per_col
    steps = chips // 2
    others = cols - 1

    fetch = pltpu.make_async_copy(dosage_ref, raw, load.at[0])
    fetch.start()
    fetch_traits = pltpu.make_async_copy(phenos_ref, traits, load.at[1])
    fetch_traits.start()

    barrier = pltpu.get_barrier_semaphore()
    for other in (upstream, sibling):
        pl.semaphore_signal(barrier, inc=1, device_id=(other, col), device_id_type=MESH)
    for k in range(1, cols):
        for other in (row, sibling):
            pl.semaphore_signal(
                barrier, inc=1, device_id=(other, (col + k) % cols), device_id_type=MESH
            )

    fetch.wait()
    values = raw[...].astype(jnp.float32)
    mean = jnp.sum(values, axis=1, keepdims=True) * (1.0 / samples)
    centred = values - mean
    var = jnp.sum(centred * centred, axis=1, keepdims=True) * (1.0 / samples)
    scale = lax.rsqrt(var + eps)

    def lanes(h):
        return pl.ds(h * part, part)

    def standard(c, h):
        lane = pl.ds(pl.multiple_of(c * wide + h * part, 128), part)
        return ((raw[:, lane].astype(jnp.float32) - mean) * scale).astype(jnp.bfloat16)

    def remote(where, there, send, recv, device):
        return pltpu.make_async_remote_copy(
            src_ref=where, dst_ref=there, send_sem=send, recv_sem=recv,
            device_id=device, device_id_type=MESH,
        )

    def piece(source, k, h):
        return pieces.at[source, (col + cols - k) % cols, :, lanes(h)]

    def swap_copy(k, h):
        return remote(
            mine.at[k - 1, :, lanes(h)], pieces.at[row, col, :, lanes(h)],
            swap_send.at[0], swap_recv.at[k - 1, h], (row, (col + k) % cols),
        )

    def first_copy(k, h):
        where = piece(row, k, h)
        return remote(where, where, first_send.at[0], first_recv.at[k, h], (sibling, col))

    def ring_copy(step, j, k, h, source):
        where = piece(source, k, h)
        return remote(
            where, where, ring_send.at[0], ring_recv.at[step, j, k, h],
            (downstream, col),
        )

    def sib_copy(h, source):
        where = col_ref.at[source, :, lanes(h)]
        return remote(where, where, sib_send.at[0], sib_recv.at[0], (sibling, col))

    def offset_of(r):
        return pl.multiple_of((r % per_col) * tall, 128)

    def line_copy(which, k, source):
        r = sibling if which else row
        return remote(
            col_ref.at[source, :, pl.ds(offset_of(r), tall)], row_ref.at[source],
            line_send.at[0], line_recv.at[0], (r, (col + k) % cols),
        )

    def share_copy(target, source):
        where = share_ref.at[col * rows + source]
        k, which = target // 2, target % 2
        return remote(
            where, where, share_send.at[0], share_recv.at[0],
            (sibling if which else row, (col + k) % cols),
        )

    def assemble(h, source):
        for c in range(cols):
            col_ref[source, c * sites:(c + 1) * sites, h * part:(h + 1) * part] = pieces[
                source, c, :, h * part:(h + 1) * part
            ]

    def spread(h, source):
        for which in (0, 1):
            @pl.when((home == col) & (offset_of(sibling if which else row) // part == h))
            def _():
                for k in range(1, cols):
                    line_copy(which, k, source).start()
        count = traits.shape[0]
        value = lax.dot_general(
            col_ref[source, :, h * part:(h + 1) * part], traits[:, h * part:(h + 1) * part],
            (((1,), (1,)), ((), ())), preferred_element_type=jnp.float32,
        )
        if h == 0:
            share_ref[col * rows + source, :, :count] = value
        else:
            share_ref[col * rows + source, :, :count] = (
                share_ref[col * rows + source, :, :count] + value
            )
        if h + 1 == halves:
            for target in range(1, 2 * cols):
                share_copy(target, source).start()

    last = steps - 1

    def arrive(step, j, k, h):
        other = core + j * (1 - 2 * core)
        if step < 0:
            source = sibling if j else row
            if j:
                first_copy(k, h).wait_recv()
            else:
                if k:
                    swap_copy(k, h).wait_recv()
                first_copy(k, h).start()
        else:
            source = row_away(step + 1, other)
            ring_copy(step, j, k, h, source).wait_recv()
        if step + 1 < last or step + 1 == last and j == 0:
            ring_copy(step + 1, j, k, h, source).start()
        if k + 1 == cols:
            assemble(h, source)
            if step >= 0:
                sib_copy(h, source).start()
            if step >= 0 or j == 0:
                spread(h, source)

    for h in range(halves):
        for k in range(1, cols):
            mine[k - 1, :, h * part:(h + 1) * part] = standard((col + k) % cols, h)
            if h == 0 and k == 1:
                pl.semaphore_wait(barrier, 2 * cols)
            swap_copy(k, h).start()
        pieces[row, col, :, h * part:(h + 1) * part] = standard(col, h)
        arrive(-1, 0, 0, h)
    for h in range(halves):
        arrive(-1, 1, 0, h)
    fetch_traits.wait()
    for stage in range(steps + cols - 1):
        for j in (0, 1):
            for h in range(halves):
                for k in range(cols):
                    step = stage - k
                    if -1 <= step < last or step == last and j == 0:
                        arrive(step, j, k, h)

    def settle(ref, semaphore):
        pltpu.make_async_copy(ref, ref, semaphore).wait()

    many = pl.ds(0, 2 * steps - 1)
    settle(col_ref.at[many], sib_recv.at[0])
    settle(share_ref.at[pl.ds(0, chips + others * rows)], share_recv.at[0])

    @pl.when(home != col)
    def _():
        settle(row_ref, line_recv.at[0])

    @pl.when(home == col)
    def _():
        for _ in range(others):
            settle(row_ref, line_send.at[0])

    settle(mine, swap_send.at[0])
    settle(pieces.at[row], first_send.at[0])
    settle(pieces.at[many], ring_send.at[0])
    settle(col_ref.at[many], sib_send.at[0])
    for _ in range(2 * cols - 1):
        settle(share_ref.at[pl.ds(0, chips)], share_send.at[0])


def product_kernel(
    rows, cols, row_ref, col_ref, share_ref, grm_ref, projected_ref, out, done,
):
    row, col = lax.axis_index("row"), lax.axis_index("col")
    sites, tall = row_ref.shape
    lines, part = out.shape[2], out.shape[3]
    parts = out.shape[1]
    per_col = rows // cols
    at_home = row // per_col == col
    offset = pl.multiple_of((row % per_col) * tall, 128)

    def write(i, j):
        return pltpu.make_async_copy(
            out.at[i % 2, j],
            grm_ref.at[pl.ds(pl.multiple_of(i * lines, lines), lines), pl.ds(j * part, part)],
            done.at[i % 2, j],
        )

    def own(start, size):
        return jnp.where(
            at_home,
            col_ref[:, pl.ds(pl.multiple_of(offset + start, 128), size)],
            row_ref[:, pl.ds(pl.multiple_of(start, 128), size)],
        )

    def step(i, carry):
        left = own(i * lines, lines)
        for j in range(parts):
            @pl.when(i >= 2)
            def _():
                write(i - 2, j).wait()
            out[i % 2, j] = lax.dot_general(
                left, col_ref[:, j * part:(j + 1) * part], (((0,), (0,)), ((), ())),
                preferred_element_type=jnp.float32,
            ) * (1.0 / sites)
            write(i, j).start()
        return carry

    count = tall // lines
    lax.fori_loop(0, count, step, 0)
    width = projected_ref.shape[1]
    share = share_ref[0]
    for c in range(1, share_ref.shape[0]):
        share = share + share_ref[c]
    projected_ref[...] = lax.dot_general(
        share[:, :projected_ref.shape[0]],
        own(col * width, width).astype(jnp.float32), (((0,), (0,)), ((), ())),
        precision=lax.Precision.HIGHEST, preferred_element_type=jnp.float32,
    ) * (1.0 / sites)
    for i in (count - 2, count - 1):
        for j in range(parts):
            write(i, j).wait()


def per_device(rows, cols, dosage, phenos):
    sites, samples = dosage.shape
    count = phenos.shape[0]
    block, wide, tall = sites * cols, samples // cols, samples // rows
    total = rows * block
    vmem = pl.BlockSpec(memory_space=pltpu.VMEM)
    anywhere = pl.BlockSpec(memory_space=pl.ANY)
    dma = pltpu.SemaphoreType.DMA
    chips = rows // 2
    steps = chips // 2
    others = cols - 1
    halves = 2
    col_block, row_block, share = pl.pallas_call(
        functools.partial(gather_kernel, rows, cols, halves),
        out_shape=[
            jax.ShapeDtypeStruct((rows, block, wide), jnp.bfloat16),
            jax.ShapeDtypeStruct((rows, block, tall), jnp.bfloat16),
            jax.ShapeDtypeStruct((cols * rows, block, 128), jnp.float32),
        ],
        in_specs=[pl.BlockSpec(memory_space=pltpu.HBM)] * 2,
        out_specs=[vmem, vmem, vmem],
        scratch_shapes=[
            pltpu.VMEM((sites, samples), jnp.bfloat16),
            pltpu.VMEM((count, wide), jnp.bfloat16),
            pltpu.VMEM((others, sites, wide), jnp.bfloat16),
            pltpu.VMEM((rows, cols, sites, wide), jnp.bfloat16),
            dma((2,)),
            dma((1,)), dma((others, halves)),
            dma((1,)), dma((cols, halves)),
            dma((1,)), dma((steps, 2, cols, halves)),
            dma((1,)), dma((1,)),
            dma((1,)), dma((1,)),
            dma((1,)), dma((1,)),
        ],
        compiler_params=pltpu.CompilerParams(
            collective_id=0, has_side_effects=True, vmem_limit_bytes=48 * 2**20
        ),
        name="gather",
    )(pltpu.with_memory_space_constraint(dosage, pltpu.HBM), pltpu.with_memory_space_constraint(phenos, pltpu.HBM))
    row_block = row_block.reshape(total, tall)
    col_block = col_block.reshape(total, wide)
    share = share.reshape(cols, total, 128)
    lines, parts = 128, 4
    grm, projected = pl.pallas_call(
        functools.partial(product_kernel, rows, cols),
        out_shape=[
            jax.ShapeDtypeStruct((tall, wide), jnp.float32),
            jax.ShapeDtypeStruct((count, tall // cols), jnp.float32),
        ],
        in_specs=[vmem, vmem, vmem],
        out_specs=[anywhere, vmem],
        scratch_shapes=[
            pltpu.VMEM((2, parts, lines, wide // parts), jnp.float32),
            dma((2, parts)),
        ],
        compiler_params=pltpu.CompilerParams(vmem_limit_bytes=48 * 2**20),
        name="product",
    )(row_block, col_block, share)
    return grm, projected


def solution(mesh):
    rows, cols = mesh.shape["row"], mesh.shape["col"]
    return jax.shard_map(
        functools.partial(per_device, rows, cols),
        mesh=mesh,
        in_specs=(P(("row", "col"), None), P(None, "col")),
        out_specs=(P("row", "col"), P(None, ("row", "col"))),
        check_vma=False,
    )
```

```python
import functools

import jax
import jax.numpy as jnp
from jax import lax
from jax.experimental import pallas as pl
from jax.experimental.pallas import tpu as pltpu
from jax.sharding import PartitionSpec as P

eps = 1e-05
MESH = pl.DeviceIdType.MESH


def place_of(row, depth, width):
    chip, core = row // 2, row % 2
    a, b = chip // width, chip % width
    turn = depth - 1 - a
    odd = turn % 2
    first = (width - 1 - b) // (width - 1)
    later = depth + turn * (width - 1) + (1 - odd) * (b - 1) + odd * (width - 1 - b)
    return first * a + (1 - first) * later, core


def chip_at(place, depth, width):
    first = 1 - jnp.minimum(place // depth, 1)
    rest = jnp.maximum(place - depth, 0)
    turn, step = rest // (width - 1), rest % (width - 1)
    odd = turn % 2
    later = (depth - 1 - turn) * width + (1 - odd) * (1 + step) + odd * (width - 1 - step)
    return first * place * width + (1 - first) * later


def gather_kernel(
    rows, cols, halves, dosage_ref, phenos_ref, col_ref, row_ref, share_ref,
    raw, traits, mine, pieces, whole,
    load, swap_send, swap_recv, first_send, first_recv, ring_send, ring_recv, sib_send, sib_recv,
    line_send, line_recv, share_send, share_recv, whole_send, inside,
):
    row, col = lax.axis_index("row"), lax.axis_index("col")
    chips = rows // 2
    depth = min(4, chips)
    width = chips // depth
    place, core = place_of(row, depth, width)
    sibling = row + 1 - 2 * core
    def row_away(shift, which):
        there = (place + (chips - shift) * (1 - core) + shift * core) % chips
        return chip_at(there, depth, width) * 2 + which

    upstream = row_away(1, core)
    downstream = row_away(chips - 1, core)
    sites, samples = dosage_ref.shape
    wide, tall = col_ref.shape[2], row_ref.shape[2]
    part = wide // halves
    per_col = rows // cols
    home = row // per_col
    steps = chips // 2
    others = cols - 1

    fetch = pltpu.make_async_copy(dosage_ref, raw, load.at[0])
    fetch.start()
    fetch_traits = pltpu.make_async_copy(phenos_ref, traits, load.at[1])
    fetch_traits.start()

    barrier = pltpu.get_barrier_semaphore()
    for other in (upstream, sibling):
        pl.semaphore_signal(barrier, inc=1, device_id=(other, col), device_id_type=MESH)
    for k in range(1, cols):
        for other in (row, sibling):
            pl.semaphore_signal(
                barrier, inc=1, device_id=(other, (col + k) % cols), device_id_type=MESH
            )

    fetch.wait()
    values = raw[...].astype(jnp.float32)
    mean = jnp.sum(values, axis=1, keepdims=True) * (1.0 / samples)
    centred = values - mean
    var = jnp.sum(centred * centred, axis=1, keepdims=True) * (1.0 / samples)
    scale = lax.rsqrt(var + eps)

    def lanes(h):
        return pl.ds(h * part, part)

    def standard(c, h):
        lane = pl.ds(pl.multiple_of(c * wide + h * part, 128), part)
        return ((raw[:, lane].astype(jnp.float32) - mean) * scale).astype(jnp.bfloat16)

    def settle(ref, semaphore):
        pltpu.make_async_copy(ref, ref, semaphore).wait()

    def remote(where, there, send, recv, device):
        return pltpu.make_async_remote_copy(
            src_ref=where, dst_ref=there, send_sem=send, recv_sem=recv,
            device_id=device, device_id_type=MESH,
        )

    def piece(source, k, h):
        return pieces.at[source, (col + cols - k) % cols, :, lanes(h)]

    def swap_copy(k, h):
        return remote(
            mine.at[k - 1, :, lanes(h)], pieces.at[row, col, :, lanes(h)],
            swap_send.at[0], swap_recv.at[k - 1, h], (row, (col + k) % cols),
        )

    def first_copy(k, h):
        where = piece(row, k, h)
        return remote(where, where, first_send.at[0], first_recv.at[k, h], (sibling, col))

    def ring_copy(step, j, k, h, source):
        where = piece(source, k, h)
        return remote(
            where, where, ring_send.at[0], ring_recv.at[step, j, k, h],
            (downstream, col),
        )

    def sib_copy(h, source):
        where = col_ref.at[source, :, lanes(h)]
        return remote(where, where, sib_send.at[0], sib_recv.at[0], (sibling, col))

    def offset_of(r):
        return pl.multiple_of((r % per_col) * tall, 128)

    def line_copy(which, k, source):
        r = sibling if which else row
        return remote(
            col_ref.at[source, :, pl.ds(offset_of(r), tall)], row_ref.at[source],
            line_send.at[0], line_recv.at[0], (r, (col + k) % cols),
        )

    def share_copy(target, source, kind=0):
        where = share_ref.at[col * rows + source]
        k, which = target // 2, target % 2
        return remote(
            where, where, share_send.at[0], share_recv.at[kind],
            (sibling if which else row, (col + k) % cols),
        )

    def whole_copy(away, which):
        return remote(
            whole, share_ref.at[col * rows + row], whole_send.at[0], share_recv.at[0],
            (row_away(away, which), col),
        )

    def assemble(h, source):
        for c in range(cols):
            col_ref[source, c * sites:(c + 1) * sites, h * part:(h + 1) * part] = pieces[
                source, c, :, h * part:(h + 1) * part
            ]

    def lines(h, source):
        for which in (0, 1):
            @pl.when((home == col) & (offset_of(sibling if which else row) // part == h))
            def _():
                for k in range(1, cols):
                    line_copy(which, k, source).start()

    def weigh(h, source, own):
        count = traits.shape[0]
        value = lax.dot_general(
            col_ref[source, :, h * part:(h + 1) * part], traits[:, h * part:(h + 1) * part],
            (((1,), (1,)), ((), ())), preferred_element_type=jnp.float32,
        )
        if h == 0:
            share_ref[col * rows + source, :, :count] = value
        else:
            share_ref[col * rows + source, :, :count] = (
                share_ref[col * rows + source, :, :count] + value
            )
        if h + 1 == halves:
            for target in range(1, 2 * cols):
                share_copy(target, source, 1 if own and target % 2 == 0 else 0).start()

    def pass_word(hop):
        if hop:
            pl.semaphore_wait(inside.at[hop - 1], 1)
        if hop < steps:
            pl.semaphore_signal(
                inside.at[hop], inc=1, device_id=(downstream, col), device_id_type=MESH
            )

    def send_whole():
        settle(share_ref.at[pl.ds(0, others)], share_recv.at[1])
        total = share_ref[row]
        for c in range(1, cols):
            total = total + share_ref[c * rows + row]
        whole[...] = total
        for away in (last, steps):
            for which in (0, 1):
                whole_copy(away, which).start()
        late = [row_away(steps, 0), row_away(steps, 1)]
        late += [row_away(last, 1 - core), row_away(chips - last, core)]
        for source in late:
            for k in range(1, cols):
                share_ref[(col + k) % cols * rows + source] = jnp.zeros(
                    share_ref.shape[1:], jnp.float32
                )

    last = steps - 1

    def arrive(step, j, k, h):
        other = core + j * (1 - 2 * core)
        if step < 0:
            source = sibling if j else row
            if j:
                first_copy(k, h).wait_recv()
            else:
                if k:
                    swap_copy(k, h).wait_recv()
                first_copy(k, h).start()
        else:
            source = row_away(step + 1, other)
            ring_copy(step, j, k, h, source).wait_recv()
        if step + 1 < last or step + 1 == last and j == 0:
            ring_copy(step + 1, j, k, h, source).start()
        if k + 1 == cols:
            assemble(h, source)
            if step >= 0:
                sib_copy(h, source).start()
            if step >= 0 or j == 0:
                lines(h, source)
            if j == 0 and step < last or j and 0 <= step < last - 1:
                weigh(h, source, step < 0)

    for h in range(halves):
        for k in range(1, cols):
            mine[k - 1, :, h * part:(h + 1) * part] = standard((col + k) % cols, h)
            if h == 0 and k == 1:
                pl.semaphore_wait(barrier, 2 * cols)
            swap_copy(k, h).start()
        pieces[row, col, :, h * part:(h + 1) * part] = standard(col, h)
        arrive(-1, 0, 0, h)
    for h in range(halves):
        arrive(-1, 1, 0, h)
    fetch_traits.wait()
    order = [
        (stage - k, j, k, h)
        for stage in range(steps + cols - 1) for j in (0, 1) for h in range(halves) for k in range(cols)
        if -1 <= stage - k < last or stage - k == last and j == 0
    ]
    begin = order.index((0, 1, cols - 1, 0))
    turns = {(hop + 1) * begin // (steps + 1): hop + 1 for hop in range(steps)}
    pass_word(0)
    for index, event in enumerate(order):
        if index in turns:
            pass_word(turns[index])
        if index == begin:
            send_whole()
        arrive(*event)

    many = pl.ds(0, 2 * steps - 1)
    settle(col_ref.at[many], sib_recv.at[0])
    settle(share_ref.at[pl.ds(0, chips + 2 + others * (rows - 5))], share_recv.at[0])

    @pl.when(home != col)
    def _():
        settle(row_ref, line_recv.at[0])

    @pl.when(home == col)
    def _():
        for _ in range(others):
            settle(row_ref, line_send.at[0])

    settle(mine, swap_send.at[0])
    settle(pieces.at[row], first_send.at[0])
    settle(pieces.at[many], ring_send.at[0])
    settle(col_ref.at[many], sib_send.at[0])
    for _ in range(2 * cols - 1):
        settle(share_ref.at[pl.ds(0, chips - 2)], share_send.at[0])
    settle(share_ref.at[pl.ds(0, 4)], whole_send.at[0])


def product_kernel(
    rows, cols, row_ref, col_ref, share_ref, grm_ref, projected_ref, out, done,
):
    row, col = lax.axis_index("row"), lax.axis_index("col")
    sites, tall = row_ref.shape
    lines, part = out.shape[2], out.shape[3]
    parts = out.shape[1]
    per_col = rows // cols
    at_home = row // per_col == col
    offset = pl.multiple_of((row % per_col) * tall, 128)

    def write(i, j):
        return pltpu.make_async_copy(
            out.at[i % 2, j],
            grm_ref.at[pl.ds(pl.multiple_of(i * lines, lines), lines), pl.ds(j * part, part)],
            done.at[i % 2, j],
        )

    def own(start, size):
        return jnp.where(
            at_home,
            col_ref[:, pl.ds(pl.multiple_of(offset + start, 128), size)],
            row_ref[:, pl.ds(pl.multiple_of(start, 128), size)],
        )

    def step(i, carry):
        left = own(i * lines, lines)
        for j in range(parts):
            @pl.when(i >= 2)
            def _():
                write(i - 2, j).wait()
            out[i % 2, j] = lax.dot_general(
                left, col_ref[:, j * part:(j + 1) * part], (((0,), (0,)), ((), ())),
                preferred_element_type=jnp.float32,
            ) * (1.0 / sites)
            write(i, j).start()
        return carry

    count = tall // lines
    lax.fori_loop(0, count, step, 0)
    width = projected_ref.shape[1]
    share = share_ref[0]
    for c in range(1, share_ref.shape[0]):
        share = share + share_ref[c]
    projected_ref[...] = lax.dot_general(
        share[:, :projected_ref.shape[0]],
        own(col * width, width).astype(jnp.float32), (((0,), (0,)), ((), ())),
        precision=lax.Precision.HIGHEST, preferred_element_type=jnp.float32,
    ) * (1.0 / sites)
    for i in (count - 2, count - 1):
        for j in range(parts):
            write(i, j).wait()


def per_device(rows, cols, dosage, phenos):
    sites, samples = dosage.shape
    count = phenos.shape[0]
    block, wide, tall = sites * cols, samples // cols, samples // rows
    total = rows * block
    vmem = pl.BlockSpec(memory_space=pltpu.VMEM)
    anywhere = pl.BlockSpec(memory_space=pl.ANY)
    dma = pltpu.SemaphoreType.DMA
    chips = rows // 2
    steps = chips // 2
    others = cols - 1
    halves = 2
    col_block, row_block, share = pl.pallas_call(
        functools.partial(gather_kernel, rows, cols, halves),
        out_shape=[
            jax.ShapeDtypeStruct((rows, block, wide), jnp.bfloat16),
            jax.ShapeDtypeStruct((rows, block, tall), jnp.bfloat16),
            jax.ShapeDtypeStruct((cols * rows, block, 128), jnp.float32),
        ],
        in_specs=[pl.BlockSpec(memory_space=pltpu.HBM)] * 2,
        out_specs=[vmem, vmem, vmem],
        scratch_shapes=[
            pltpu.VMEM((sites, samples), jnp.bfloat16),
            pltpu.VMEM((count, wide), jnp.bfloat16),
            pltpu.VMEM((others, sites, wide), jnp.bfloat16),
            pltpu.VMEM((rows, cols, sites, wide), jnp.bfloat16),
            pltpu.VMEM((block, 128), jnp.float32),
            dma((2,)),
            dma((1,)), dma((others, halves)),
            dma((1,)), dma((cols, halves)),
            dma((1,)), dma((steps, 2, cols, halves)),
            dma((1,)), dma((1,)),
            dma((1,)), dma((1,)),
            dma((1,)), dma((2,)),
            dma((1,)), pltpu.SemaphoreType.REGULAR((steps,)),
        ],
        compiler_params=pltpu.CompilerParams(
            collective_id=0, has_side_effects=True, vmem_limit_bytes=48 * 2**20
        ),
        name="gather",
    )(pltpu.with_memory_space_constraint(dosage, pltpu.HBM), pltpu.with_memory_space_constraint(phenos, pltpu.HBM))
    row_block = row_block.reshape(total, tall)
    col_block = col_block.reshape(total, wide)
    share = share.reshape(cols, total, 128)
    lines, parts = 128, 4
    grm, projected = pl.pallas_call(
        functools.partial(product_kernel, rows, cols),
        out_shape=[
            jax.ShapeDtypeStruct((tall, wide), jnp.float32),
            jax.ShapeDtypeStruct((count, tall // cols), jnp.float32),
        ],
        in_specs=[vmem, vmem, vmem],
        out_specs=[anywhere, vmem],
        scratch_shapes=[
            pltpu.VMEM((2, parts, lines, wide // parts), jnp.float32),
            dma((2, parts)),
        ],
        compiler_params=pltpu.CompilerParams(vmem_limit_bytes=48 * 2**20),
        name="product",
    )(row_block, col_block, share)
    return grm, projected


def solution(mesh):
    rows, cols = mesh.shape["row"], mesh.shape["col"]
    return jax.shard_map(
        functools.partial(per_device, rows, cols),
        mesh=mesh,
        in_specs=(P(("row", "col"), None), P(None, "col")),
        out_specs=(P("row", "col"), P(None, ("row", "col"))),
        check_vma=False,
    )
```

```python
import functools

import jax
import jax.numpy as jnp
from jax import lax
from jax.experimental import pallas as pl
from jax.experimental.pallas import tpu as pltpu
from jax.sharding import PartitionSpec as P

eps = 1e-05
MESH = pl.DeviceIdType.MESH


def place_of(row, depth, width):
    chip, core = row // 2, row % 2
    a, b = chip // width, chip % width
    turn = depth - 1 - a
    odd = turn % 2
    first = (width - 1 - b) // (width - 1)
    later = depth + turn * (width - 1) + (1 - odd) * (b - 1) + odd * (width - 1 - b)
    return first * a + (1 - first) * later, core


def chip_at(place, depth, width):
    first = 1 - jnp.minimum(place // depth, 1)
    rest = jnp.maximum(place - depth, 0)
    turn, step = rest // (width - 1), rest % (width - 1)
    odd = turn % 2
    later = (depth - 1 - turn) * width + (1 - odd) * (1 + step) + odd * (width - 1 - step)
    return first * place * width + (1 - first) * later


def gather_kernel(
    rows, cols, halves, dosage_ref, phenos_ref, col_ref, row_ref, share_ref,
    raw, traits, mine, pieces, whole,
    load, swap_send, swap_recv, first_send, first_recv, ring_send, ring_recv, sib_send, sib_recv,
    line_send, line_recv, share_send, share_recv, whole_send, inside,
):
    row, col = lax.axis_index("row"), lax.axis_index("col")
    chips = rows // 2
    depth = min(4, chips)
    width = chips // depth
    place, core = place_of(row, depth, width)
    sibling = row + 1 - 2 * core
    def row_away(shift, which):
        there = (place + (chips - shift) * (1 - core) + shift * core) % chips
        return chip_at(there, depth, width) * 2 + which

    upstream = row_away(1, core)
    downstream = row_away(chips - 1, core)
    sites, samples = dosage_ref.shape
    wide, tall = col_ref.shape[2], row_ref.shape[2]
    part = wide // halves
    per_col = rows // cols
    home = row // per_col
    steps = chips // 2
    others = cols - 1

    quarter = samples // 4
    spans = [pl.ds(q * quarter, quarter) for q in range(4)]
    fetches = [
        pltpu.make_async_copy(dosage_ref.at[:, span], raw.at[:, span], load.at[1 + q])
        for q, span in enumerate(spans)
    ]
    for fetch in fetches:
        fetch.start()
    fetch_traits = pltpu.make_async_copy(phenos_ref, traits, load.at[0])
    fetch_traits.start()

    barrier = pltpu.get_barrier_semaphore()
    for other in (upstream, sibling):
        pl.semaphore_signal(barrier, inc=1, device_id=(other, col), device_id_type=MESH)
    for k in range(1, cols):
        for other in (row, sibling):
            pl.semaphore_signal(
                barrier, inc=1, device_id=(other, (col + k) % cols), device_id_type=MESH
            )

    mean = jnp.zeros((sites, 128), jnp.float32)
    for fetch, span in zip(fetches, spans):
        fetch.wait()
        values = raw[:, span].astype(jnp.float32)
        mean = mean + jnp.sum(values.reshape(sites, quarter // 128, 128), axis=1)
    mean = jnp.sum(mean, axis=1, keepdims=True) * (1.0 / samples)
    centred = raw[...].astype(jnp.float32) - mean
    var = jnp.sum(centred * centred, axis=1, keepdims=True) * (1.0 / samples)
    scale = lax.rsqrt(var + eps)

    def lanes(h):
        return pl.ds(h * part, part)

    def standard(c, h):
        lane = pl.ds(pl.multiple_of(c * wide + h * part, 128), part)
        return ((raw[:, lane].astype(jnp.float32) - mean) * scale).astype(jnp.bfloat16)

    def settle(ref, semaphore):
        pltpu.make_async_copy(ref, ref, semaphore).wait()

    def remote(where, there, send, recv, device):
        return pltpu.make_async_remote_copy(
            src_ref=where, dst_ref=there, send_sem=send, recv_sem=recv,
            device_id=device, device_id_type=MESH,
        )

    def piece(source, k, h):
        return pieces.at[source, (col + cols - k) % cols, :, lanes(h)]

    def swap_copy(k, h):
        return remote(
            mine.at[k - 1, :, lanes(h)], pieces.at[row, col, :, lanes(h)],
            swap_send.at[0], swap_recv.at[k - 1, h], (row, (col + k) % cols),
        )

    def first_copy(k, h):
        where = piece(row, k, h)
        return remote(where, where, first_send.at[0], first_recv.at[k, h], (sibling, col))

    def ring_copy(step, j, k, h, source):
        where = piece(source, k, h)
        return remote(
            where, where, ring_send.at[0], ring_recv.at[step, j, k, h],
            (downstream, col),
        )

    def sib_copy(h, source):
        where = col_ref.at[source, :, lanes(h)]
        return remote(where, where, sib_send.at[0], sib_recv.at[0], (sibling, col))

    def offset_of(r):
        return pl.multiple_of((r % per_col) * tall, 128)

    def line_copy(which, k, source):
        r = sibling if which else row
        return remote(
            col_ref.at[source, :, pl.ds(offset_of(r), tall)], row_ref.at[source],
            line_send.at[0], line_recv.at[0], (r, (col + k) % cols),
        )

    def share_copy(target, source, kind=0):
        where = share_ref.at[col * rows + source]
        k, which = target // 2, target % 2
        return remote(
            where, where, share_send.at[0], share_recv.at[kind],
            (sibling if which else row, (col + k) % cols),
        )

    def whole_copy(away, which):
        return remote(
            whole, share_ref.at[col * rows + row], whole_send.at[0], share_recv.at[0],
            (row_away(away, which), col),
        )

    def assemble(h, source):
        for c in range(cols):
            col_ref[source, c * sites:(c + 1) * sites, h * part:(h + 1) * part] = pieces[
                source, c, :, h * part:(h + 1) * part
            ]

    def lines(h, source):
        for which in (0, 1):
            @pl.when((home == col) & (offset_of(sibling if which else row) // part == h))
            def _():
                for k in range(1, cols):
                    line_copy(which, k, source).start()

    def weigh(h, source, own):
        count = traits.shape[0]
        value = lax.dot_general(
            col_ref[source, :, h * part:(h + 1) * part], traits[:, h * part:(h + 1) * part],
            (((1,), (1,)), ((), ())), preferred_element_type=jnp.float32,
        )
        if h == 0:
            share_ref[col * rows + source, :, :count] = value
        else:
            share_ref[col * rows + source, :, :count] = (
                share_ref[col * rows + source, :, :count] + value
            )
        if h + 1 == halves:
            for target in range(1, 2 * cols):
                share_copy(target, source, 1 if own and target % 2 == 0 else 0).start()

    def pass_word(hop):
        if hop:
            pl.semaphore_wait(inside.at[hop - 1], 1)
        if hop < steps:
            pl.semaphore_signal(
                inside.at[hop], inc=1, device_id=(downstream, col), device_id_type=MESH
            )

    def send_whole():
        settle(share_ref.at[pl.ds(0, others)], share_recv.at[1])
        total = share_ref[row]
        for c in range(1, cols):
            total = total + share_ref[c * rows + row]
        whole[...] = total
        for away in (last, steps):
            for which in (0, 1):
                whole_copy(away, which).start()
        late = [row_away(steps, 0), row_away(steps, 1)]
        late += [row_away(last, 1 - core), row_away(chips - last, core)]
        for source in late:
            for k in range(1, cols):
                share_ref[(col + k) % cols * rows + source] = jnp.zeros(
                    share_ref.shape[1:], jnp.float32
                )

    last = steps - 1

    def arrive(step, j, k, h):
        other = core + j * (1 - 2 * core)
        if step < 0:
            source = sibling if j else row
            if j:
                first_copy(k, h).wait_recv()
            else:
                if k:
                    swap_copy(k, h).wait_recv()
                first_copy(k, h).start()
        else:
            source = row_away(step + 1, other)
            ring_copy(step, j, k, h, source).wait_recv()
        if step + 1 < last or step + 1 == last and j == 0:
            ring_copy(step + 1, j, k, h, source).start()
        if k + 1 == cols:
            assemble(h, source)
            if step >= 0:
                sib_copy(h, source).start()
            if step >= 0 or j == 0:
                lines(h, source)
            if j == 0 and step < last or j and 0 <= step < last - 1:
                weigh(h, source, step < 0)

    for h in range(halves):
        for k in range(1, cols):
            mine[k - 1, :, h * part:(h + 1) * part] = standard((col + k) % cols, h)
            if h == 0 and k == 1:
                pl.semaphore_wait(barrier, 2 * cols)
            swap_copy(k, h).start()
        pieces[row, col, :, h * part:(h + 1) * part] = standard(col, h)
        arrive(-1, 0, 0, h)
    for h in range(halves):
        arrive(-1, 1, 0, h)
    fetch_traits.wait()
    order = []
    for stage in range(steps + cols - 1):
        for j in (0, 1):
            turn = [(h, k) for h in range(halves) for k in reversed(range(cols))] if stage == 0 else [(h, k) for h in range(halves) for k in range(cols)] if stage < cols else [(h, k) for k in reversed(range(cols)) for h in range(halves)]
            for h, k in turn:
                step = stage - k
                if -1 <= step < last or step == last and j == 0:
                    order.append((step, j, k, h))
    begin = order.index((0, 1, cols - 1, 0))
    turns = {(hop + 1) * begin // (steps + 1): hop + 1 for hop in range(steps)}
    pass_word(0)
    for index, event in enumerate(order):
        if index in turns:
            pass_word(turns[index])
        if index == begin:
            send_whole()
        arrive(*event)

    many = pl.ds(0, 2 * steps - 1)
    settle(col_ref.at[many], sib_recv.at[0])
    settle(share_ref.at[pl.ds(0, chips + 2 + others * (rows - 5))], share_recv.at[0])

    @pl.when(home != col)
    def _():
        settle(row_ref, line_recv.at[0])

    @pl.when(home == col)
    def _():
        for _ in range(others):
            settle(row_ref, line_send.at[0])

    settle(mine, swap_send.at[0])
    settle(pieces.at[row], first_send.at[0])
    settle(pieces.at[many], ring_send.at[0])
    settle(col_ref.at[many], sib_send.at[0])
    for _ in range(2 * cols - 1):
        settle(share_ref.at[pl.ds(0, chips - 2)], share_send.at[0])
    settle(share_ref.at[pl.ds(0, 4)], whole_send.at[0])


def product_kernel(
    rows, cols, row_ref, col_ref, share_ref, grm_ref, projected_ref, out, done,
):
    row, col = lax.axis_index("row"), lax.axis_index("col")
    sites, tall = row_ref.shape
    lines, part = out.shape[2], out.shape[3]
    parts = out.shape[1]
    per_col = rows // cols
    at_home = row // per_col == col
    offset = pl.multiple_of((row % per_col) * tall, 128)

    def write(i, j):
        return pltpu.make_async_copy(
            out.at[i % 2, j],
            grm_ref.at[pl.ds(pl.multiple_of(i * lines, lines), lines), pl.ds(j * part, part)],
            done.at[i % 2, j],
        )

    def own(start, size):
        return jnp.where(
            at_home,
            col_ref[:, pl.ds(pl.multiple_of(offset + start, 128), size)],
            row_ref[:, pl.ds(pl.multiple_of(start, 128), size)],
        )

    def step(i, carry):
        left = own(i * lines, lines)
        for j in range(parts):
            @pl.when(i >= 2)
            def _():
                write(i - 2, j).wait()
            out[i % 2, j] = lax.dot_general(
                left, col_ref[:, j * part:(j + 1) * part], (((0,), (0,)), ((), ())),
                preferred_element_type=jnp.float32,
            ) * (1.0 / sites)
            write(i, j).start()
        return carry

    count = tall // lines
    lax.fori_loop(0, count, step, 0)
    width = projected_ref.shape[1]
    share = share_ref[0]
    for c in range(1, share_ref.shape[0]):
        share = share + share_ref[c]
    projected_ref[...] = lax.dot_general(
        share[:, :projected_ref.shape[0]],
        own(col * width, width).astype(jnp.float32), (((0,), (0,)), ((), ())),
        precision=lax.Precision.HIGHEST, preferred_element_type=jnp.float32,
    ) * (1.0 / sites)
    for i in (count - 2, count - 1):
        for j in range(parts):
            write(i, j).wait()


def per_device(rows, cols, dosage, phenos):
    sites, samples = dosage.shape
    count = phenos.shape[0]
    block, wide, tall = sites * cols, samples // cols, samples // rows
    total = rows * block
    vmem = pl.BlockSpec(memory_space=pltpu.VMEM)
    anywhere = pl.BlockSpec(memory_space=pl.ANY)
    dma = pltpu.SemaphoreType.DMA
    chips = rows // 2
    steps = chips // 2
    others = cols - 1
    halves = 4
    col_block, row_block, share = pl.pallas_call(
        functools.partial(gather_kernel, rows, cols, halves),
        out_shape=[
            jax.ShapeDtypeStruct((rows, block, wide), jnp.bfloat16),
            jax.ShapeDtypeStruct((rows, block, tall), jnp.bfloat16),
            jax.ShapeDtypeStruct((cols * rows, block, 128), jnp.float32),
        ],
        in_specs=[pl.BlockSpec(memory_space=pltpu.HBM)] * 2,
        out_specs=[vmem, vmem, vmem],
        scratch_shapes=[
            pltpu.VMEM((sites, samples), jnp.bfloat16),
            pltpu.VMEM((count, wide), jnp.bfloat16),
            pltpu.VMEM((others, sites, wide), jnp.bfloat16),
            pltpu.VMEM((rows, cols, sites, wide), jnp.bfloat16),
            pltpu.VMEM((block, 128), jnp.float32),
            dma((5,)),
            dma((1,)), dma((others, halves)),
            dma((1,)), dma((cols, halves)),
            dma((1,)), dma((steps, 2, cols, halves)),
            dma((1,)), dma((1,)),
            dma((1,)), dma((1,)),
            dma((1,)), dma((2,)),
            dma((1,)), pltpu.SemaphoreType.REGULAR((steps,)),
        ],
        compiler_params=pltpu.CompilerParams(
            collective_id=0, has_side_effects=True, vmem_limit_bytes=48 * 2**20
        ),
        name="gather",
    )(pltpu.with_memory_space_constraint(dosage, pltpu.HBM), pltpu.with_memory_space_constraint(phenos, pltpu.HBM))
    row_block = row_block.reshape(total, tall)
    col_block = col_block.reshape(total, wide)
    share = share.reshape(cols, total, 128)
    lines, parts = 128, 4
    grm, projected = pl.pallas_call(
        functools.partial(product_kernel, rows, cols),
        out_shape=[
            jax.ShapeDtypeStruct((tall, wide), jnp.float32),
            jax.ShapeDtypeStruct((count, tall // cols), jnp.float32),
        ],
        in_specs=[vmem, vmem, vmem],
        out_specs=[anywhere, vmem],
        scratch_shapes=[
            pltpu.VMEM((2, parts, lines, wide // parts), jnp.float32),
            dma((2, parts)),
        ],
        compiler_params=pltpu.CompilerParams(vmem_limit_bytes=48 * 2**20),
        name="product",
    )(row_block, col_block, share)
    return grm, projected


def solution(mesh):
    rows, cols = mesh.shape["row"], mesh.shape["col"]
    return jax.shard_map(
        functools.partial(per_device, rows, cols),
        mesh=mesh,
        in_specs=(P(("row", "col"), None), P(None, "col")),
        out_specs=(P("row", "col"), P(None, ("row", "col"))),
        check_vma=False,
    )
```

```python
import functools

import jax
import jax.numpy as jnp
from jax import lax
from jax.experimental import pallas as pl
from jax.experimental.pallas import tpu as pltpu
from jax.sharding import PartitionSpec as P

eps = 1e-05
MESH = pl.DeviceIdType.MESH


def place_of(row, depth, width):
    chip, core = row // 2, row % 2
    a, b = chip // width, chip % width
    turn = depth - 1 - a
    odd = turn % 2
    first = (width - 1 - b) // (width - 1)
    later = depth + turn * (width - 1) + (1 - odd) * (b - 1) + odd * (width - 1 - b)
    return first * a + (1 - first) * later, core


def chip_at(place, depth, width):
    first = 1 - jnp.minimum(place // depth, 1)
    rest = jnp.maximum(place - depth, 0)
    turn, step = rest // (width - 1), rest % (width - 1)
    odd = turn % 2
    later = (depth - 1 - turn) * width + (1 - odd) * (1 + step) + odd * (width - 1 - step)
    return first * place * width + (1 - first) * later


def gather_kernel(
    rows, cols, halves, dosage_ref, phenos_ref, col_ref, row_ref, share_ref,
    raw, traits, mine, pieces, whole,
    load, swap_send, swap_recv, first_send, first_recv, ring_send, ring_recv, sib_send, sib_recv,
    line_send, line_recv, share_send, share_recv, whole_send, inside,
):
    row, col = lax.axis_index("row"), lax.axis_index("col")
    chips = rows // 2
    depth = min(4, chips)
    width = chips // depth
    place, core = place_of(row, depth, width)
    sibling = row + 1 - 2 * core
    def row_away(shift, which):
        there = (place + (chips - shift) * (1 - core) + shift * core) % chips
        return chip_at(there, depth, width) * 2 + which

    upstream = row_away(1, core)
    downstream = row_away(chips - 1, core)
    sites, samples = dosage_ref.shape
    wide, tall = col_ref.shape[2], row_ref.shape[2]
    part = wide // halves
    per_col = rows // cols
    home = row // per_col
    steps = chips // 2
    others = cols - 1

    quarter = samples // 4
    spans = [pl.ds(q * quarter, quarter) for q in range(4)]
    fetches = [
        pltpu.make_async_copy(dosage_ref.at[:, span], raw.at[:, span], load.at[1 + q])
        for q, span in enumerate(spans)
    ]
    for fetch in fetches:
        fetch.start()
    fetch_traits = pltpu.make_async_copy(phenos_ref, traits, load.at[0])
    fetch_traits.start()

    barrier = pltpu.get_barrier_semaphore()
    for other in (upstream, sibling):
        pl.semaphore_signal(barrier, inc=1, device_id=(other, col), device_id_type=MESH)
    for k in range(1, cols):
        for other in (row, sibling):
            pl.semaphore_signal(
                barrier, inc=1, device_id=(other, (col + k) % cols), device_id_type=MESH
            )

    mean = jnp.zeros((sites, 128), jnp.float32)
    for fetch, span in zip(fetches, spans):
        fetch.wait()
        values = raw[:, span].astype(jnp.float32)
        mean = mean + jnp.sum(values.reshape(sites, quarter // 128, 128), axis=1)
    mean = jnp.sum(mean, axis=1, keepdims=True) * (1.0 / samples)
    centred = raw[...].astype(jnp.float32) - mean
    var = jnp.sum(centred * centred, axis=1, keepdims=True) * (1.0 / samples)
    scale = lax.rsqrt(var + eps)

    def lanes(h):
        return pl.ds(h * part, part)

    def standard(c, h):
        lane = pl.ds(pl.multiple_of(c * wide + h * part, 128), part)
        return ((raw[:, lane].astype(jnp.float32) - mean) * scale).astype(jnp.bfloat16)

    def settle(ref, semaphore):
        pltpu.make_async_copy(ref, ref, semaphore).wait()

    def remote(where, there, send, recv, device):
        return pltpu.make_async_remote_copy(
            src_ref=where, dst_ref=there, send_sem=send, recv_sem=recv,
            device_id=device, device_id_type=MESH,
        )

    def piece(source, k, h):
        return pieces.at[source, (col + cols - k) % cols, :, lanes(h)]

    def swap_copy(k, h):
        return remote(
            mine.at[k - 1, :, lanes(h)], pieces.at[row, col, :, lanes(h)],
            swap_send.at[0], swap_recv.at[k - 1, h], (row, (col + k) % cols),
        )

    def first_copy(k, h):
        where = piece(row, k, h)
        return remote(where, where, first_send.at[0], first_recv.at[k, h], (sibling, col))

    def ring_copy(step, j, k, h, source):
        where = piece(source, k, h)
        return remote(
            where, where, ring_send.at[0], ring_recv.at[step, j, k, h],
            (downstream, col),
        )

    def sib_copy(h, source):
        where = col_ref.at[source, :, lanes(h)]
        return remote(where, where, sib_send.at[0], sib_recv.at[0], (sibling, col))

    def offset_of(r):
        return pl.multiple_of((r % per_col) * tall, 128)

    def line_copy(which, k, source):
        r = sibling if which else row
        return remote(
            col_ref.at[source, :, pl.ds(offset_of(r), tall)], row_ref.at[source],
            line_send.at[0], line_recv.at[0], (r, (col + k) % cols),
        )

    def share_copy(target, source, kind=0):
        where = share_ref.at[col * rows + source]
        k, which = target // 2, target % 2
        return remote(
            where, where, share_send.at[0], share_recv.at[kind],
            (sibling if which else row, (col + k) % cols),
        )

    def whole_copy(away, which):
        return remote(
            whole, share_ref.at[col * rows + row], whole_send.at[0], share_recv.at[0],
            (row_away(away, which), col),
        )

    def assemble(h, source):
        for c in range(cols):
            col_ref[source, c * sites:(c + 1) * sites, h * part:(h + 1) * part] = pieces[
                source, c, :, h * part:(h + 1) * part
            ]

    def lines(h, source):
        for which in (0, 1):
            @pl.when((home == col) & (offset_of(sibling if which else row) // part == h))
            def _():
                for k in range(1, cols):
                    line_copy(which, k, source).start()

    def weigh(h, source, own):
        count = traits.shape[0]
        value = lax.dot_general(
            col_ref[source, :, h * part:(h + 1) * part], traits[:, h * part:(h + 1) * part],
            (((1,), (1,)), ((), ())), preferred_element_type=jnp.float32,
        )
        if h == 0:
            share_ref[col * rows + source, :, :count] = value
        else:
            share_ref[col * rows + source, :, :count] = (
                share_ref[col * rows + source, :, :count] + value
            )
        if h + 1 == halves:
            for target in range(1, 2 * cols):
                share_copy(target, source, 1 if own and target % 2 == 0 else 0).start()

    def pass_word(hop):
        if hop:
            pl.semaphore_wait(inside.at[hop - 1], 1)
        if hop < steps:
            pl.semaphore_signal(
                inside.at[hop], inc=1, device_id=(downstream, col), device_id_type=MESH
            )

    def send_whole():
        settle(share_ref.at[pl.ds(0, others)], share_recv.at[1])
        total = share_ref[row]
        for c in range(1, cols):
            total = total + share_ref[c * rows + row]
        whole[...] = total
        for away in (last, steps):
            for which in (0, 1):
                whole_copy(away, which).start()
        late = [row_away(steps, 0), row_away(steps, 1)]
        late += [row_away(last, 1 - core), row_away(chips - last, core)]
        for source in late:
            for k in range(1, cols):
                share_ref[(col + k) % cols * rows + source] = jnp.zeros(
                    share_ref.shape[1:], jnp.float32
                )

    last = steps - 1

    def arrive(step, j, k, h):
        other = core + j * (1 - 2 * core)
        if step < 0:
            source = sibling if j else row
            if j:
                first_copy(k, h).wait_recv()
            else:
                if k:
                    swap_copy(k, h).wait_recv()
                first_copy(k, h).start()
        else:
            source = row_away(step + 1, other)
            ring_copy(step, j, k, h, source).wait_recv()
        if step + 1 < last or step + 1 == last and j == 0:
            ring_copy(step + 1, j, k, h, source).start()
        if k + 1 == cols:
            assemble(h, source)
            if step >= 0:
                sib_copy(h, source).start()
            if step >= 0 or j == 0:
                lines(h, source)
            if j == 0 and step < last or j and 0 <= step < last - 1:
                weigh(h, source, step < 0)

    for h in range(halves):
        for k in range(1, cols):
            mine[k - 1, :, h * part:(h + 1) * part] = standard((col + k) % cols, h)
            if h == 0 and k == 1:
                pl.semaphore_wait(barrier, 2 * cols)
            swap_copy(k, h).start()
        pieces[row, col, :, h * part:(h + 1) * part] = standard(col, h)
        arrive(-1, 0, 0, h)
    for h in range(halves):
        arrive(-1, 1, 0, h)
    fetch_traits.wait()
    order = []
    for stage in range(steps + cols - 1):
        for j in (0, 1):
            turn = [(h, k) for h in range(halves) for k in reversed(range(cols))] if stage == 0 else [(h, k) for h in range(halves) for k in range(cols)] if stage < cols else [(h, k) for k in reversed(range(cols)) for h in range(halves)]
            for h, k in turn:
                step = stage - k
                if -1 <= step < last or step == last and j == 0:
                    order.append((step, j, k, h))
    begin = order.index((0, 1, cols - 1, 0))
    turns = {(hop + 1) * begin // (steps + 1): hop + 1 for hop in range(steps)}
    pass_word(0)
    for index, event in enumerate(order):
        if index in turns:
            pass_word(turns[index])
        if index == begin:
            send_whole()
        arrive(*event)

    many = pl.ds(0, 2 * steps - 1)
    settle(col_ref.at[many], sib_recv.at[0])
    settle(share_ref.at[pl.ds(0, chips + 2 + others * (rows - 5))], share_recv.at[0])

    @pl.when(home != col)
    def _():
        settle(row_ref, line_recv.at[0])

    @pl.when(home == col)
    def _():
        for _ in range(others):
            settle(row_ref, line_send.at[0])

    settle(mine, swap_send.at[0])
    settle(pieces.at[row], first_send.at[0])
    settle(pieces.at[many], ring_send.at[0])
    settle(col_ref.at[many], sib_send.at[0])
    for _ in range(2 * cols - 1):
        settle(share_ref.at[pl.ds(0, chips - 2)], share_send.at[0])
    settle(share_ref.at[pl.ds(0, 4)], whole_send.at[0])


def product_kernel(
    rows, cols, row_ref, col_ref, share_ref, grm_ref, projected_ref, out, done,
):
    row, col = lax.axis_index("row"), lax.axis_index("col")
    sites, tall = row_ref.shape
    lines, part = out.shape[2], out.shape[3]
    parts = out.shape[1]
    per_col = rows // cols
    at_home = row // per_col == col
    offset = pl.multiple_of((row % per_col) * tall, 128)

    def write(i, j):
        return pltpu.make_async_copy(
            out.at[i % 2, j],
            grm_ref.at[pl.ds(pl.multiple_of(i * lines, lines), lines), pl.ds(j * part, part)],
            done.at[i % 2, j],
        )

    def own(start, size):
        return jnp.where(
            at_home,
            col_ref[:, pl.ds(pl.multiple_of(offset + start, 128), size)],
            row_ref[:, pl.ds(pl.multiple_of(start, 128), size)],
        )

    def tile(left, start, size):
        return lax.dot_general(
            left, col_ref[:, start:start + size], (((0,), (0,)), ((), ())),
            preferred_element_type=jnp.float32,
        ) * (1.0 / sites)

    def step(i, carry):
        left = own(i * lines, lines)
        for j in range(parts):
            @pl.when(i >= 2)
            def _():
                write(i - 2, j).wait()
            out[i % 2, j] = tile(left, j * part, part)
            write(i, j).start()
        return carry

    left = own(0, lines)
    piece = part // 6
    for j in range(parts):
        for start in range(0, part, piece):
            out[0, j, :, start:start + piece] = tile(left, j * part + start, piece)
            pltpu.make_async_copy(
                out.at[0, j, :, pl.ds(start, piece)],
                grm_ref.at[pl.ds(0, lines), pl.ds(j * part + start, piece)],
                done.at[0, j],
            ).start()
    count = tall // lines
    lax.fori_loop(1, count, step, 0)
    width = projected_ref.shape[1]
    share = share_ref[0]
    for c in range(1, share_ref.shape[0]):
        share = share + share_ref[c]
    projected_ref[...] = lax.dot_general(
        share[:, :projected_ref.shape[0]],
        own(col * width, width).astype(jnp.float32), (((0,), (0,)), ((), ())),
        precision=lax.Precision.HIGHEST, preferred_element_type=jnp.float32,
    ) * (1.0 / sites)
    for i in (count - 2, count - 1):
        for j in range(parts):
            write(i, j).wait()


def per_device(rows, cols, dosage, phenos):
    sites, samples = dosage.shape
    count = phenos.shape[0]
    block, wide, tall = sites * cols, samples // cols, samples // rows
    total = rows * block
    vmem = pl.BlockSpec(memory_space=pltpu.VMEM)
    anywhere = pl.BlockSpec(memory_space=pl.ANY)
    dma = pltpu.SemaphoreType.DMA
    chips = rows // 2
    steps = chips // 2
    others = cols - 1
    halves = 4
    col_block, row_block, share = pl.pallas_call(
        functools.partial(gather_kernel, rows, cols, halves),
        out_shape=[
            jax.ShapeDtypeStruct((rows, block, wide), jnp.bfloat16),
            jax.ShapeDtypeStruct((rows, block, tall), jnp.bfloat16),
            jax.ShapeDtypeStruct((cols * rows, block, 128), jnp.float32),
        ],
        in_specs=[pl.BlockSpec(memory_space=pltpu.HBM)] * 2,
        out_specs=[vmem, vmem, vmem],
        scratch_shapes=[
            pltpu.VMEM((sites, samples), jnp.bfloat16),
            pltpu.VMEM((count, wide), jnp.bfloat16),
            pltpu.VMEM((others, sites, wide), jnp.bfloat16),
            pltpu.VMEM((rows, cols, sites, wide), jnp.bfloat16),
            pltpu.VMEM((block, 128), jnp.float32),
            dma((5,)),
            dma((1,)), dma((others, halves)),
            dma((1,)), dma((cols, halves)),
            dma((1,)), dma((steps, 2, cols, halves)),
            dma((1,)), dma((1,)),
            dma((1,)), dma((1,)),
            dma((1,)), dma((2,)),
            dma((1,)), pltpu.SemaphoreType.REGULAR((steps,)),
        ],
        compiler_params=pltpu.CompilerParams(
            collective_id=0, has_side_effects=True, vmem_limit_bytes=48 * 2**20
        ),
        name="gather",
    )(pltpu.with_memory_space_constraint(dosage, pltpu.HBM), pltpu.with_memory_space_constraint(phenos, pltpu.HBM))
    row_block = row_block.reshape(total, tall)
    col_block = col_block.reshape(total, wide)
    share = share.reshape(cols, total, 128)
    lines, parts = 128, 4
    grm, projected = pl.pallas_call(
        functools.partial(product_kernel, rows, cols),
        out_shape=[
            jax.ShapeDtypeStruct((tall, wide), jnp.float32),
            jax.ShapeDtypeStruct((count, tall // cols), jnp.float32),
        ],
        in_specs=[vmem, vmem, vmem],
        out_specs=[anywhere, vmem],
        scratch_shapes=[
            pltpu.VMEM((2, parts, lines, wide // parts), jnp.float32),
            dma((2, parts)),
        ],
        compiler_params=pltpu.CompilerParams(vmem_limit_bytes=48 * 2**20),
        name="product",
    )(row_block, col_block, share)
    return grm, projected


def solution(mesh):
    rows, cols = mesh.shape["row"], mesh.shape["col"]
    return jax.shard_map(
        functools.partial(per_device, rows, cols),
        mesh=mesh,
        in_specs=(P(("row", "col"), None), P(None, "col")),
        out_specs=(P("row", "col"), P(None, ("row", "col"))),
        check_vma=False,
    )
```
